32 devices in a mesh: seq: 4 (over y, x), dp: 4 (over z), enc: 2 (over core).
Axes of the slice: x: 2, y: 2, z: 4, core: 2. Of those that a mesh axis runs over, the one named last changes fastest.
Arguments:
- lm_grad: bfloat16 [4, 4, 192, 1152], P('dp', 'enc', 'seq'), may hold values from -6 to 6
- image_tokens: int32 [4, 4, 4], P('dp'), may hold values from 1 to 15, as said below
- image_offset: int32 [4, 4, 4], P('dp'), may hold values from 0 to 47, as said below
- image_owner: int32 [4, 4, 4], P('dp'), may hold values from 0 to 3, as said below
- mlp_input: bfloat16 [4, 4, 240, 1152], P('dp', None, 'seq'), may hold values from -36 to 36
- layer_output: bfloat16 [4, 4, 240, 1152], P('dp', 'enc', 'seq'), may hold values from -36 to 36
- pre_gain: float32 [1152], replicated, may hold values from 0.5 to 1.5
- pre_bias: float32 [1152], replicated, may hold values from -3 to 3
- fc1_weight: bfloat16 [1152, 4304], P(None, 'enc'), may hold values from -0.1875 to 0.1875
- fc1_bias: float32 [4304], P('enc'), may hold values from -3 to 3
- fc2_weight: bfloat16 [4304, 1152], P('enc'), may hold values from -0.09375 to 0.09375
- post_gain: float32 [1152], replicated, may hold values from 0.5 to 1.5
- post_bias: float32 [1152], replicated, may hold values from -3 to 3
- merge_gain: float32 [1152], replicated, may hold values from 0.5 to 1.5
Outputs:
- act_grad: bfloat16 [4, 4, 240, 1152], P('dp', 'enc', 'seq')
- norm_grads: float32 [6, 1152], replicated
- fc1_bias_grad: float32 [4304], replicated
The draws below stay inside these ranges and needn't reach their ends.
Inputs may be any that keep to these rules, and one draw needn't show every extreme that they name: `image_tokens`: the 4 images of one LM shard have token counts that sum to 48, and one of them has 15. `image_offset`: the images of one LM shard lie back to back over its 48 rows, in some order; each entry is an image's first row in its shard. Images are placed round-robin by their index j in a shard: image_owner[r, q, j] = (q + image_owner[r, 0, j]) mod 4, with the 4 values image_owner[r, 0, j] different. So each encoder chip owns exactly 4 images of its replica, the visual tokens owned by one chip number at most 60, and some chip owns exactly 60.
All inputs are finite; a program needn't handle non-finite values.
Results may differ from the reference program's by a relative error of at most 0.005.
Values may be sent and summed in bfloat16 or wider, within the bound.
A program may use at most 64 MiB of HBM per device.

```python
import math
import jax
import jax.numpy as jnp
from jax import lax

D = 1152
FF = 4304
PATCH_GROUP = 4
IMG_SHARD = 4
MOST_LEN = 15
ROWS_DEV = 48
CAP_TOK = 60
SHARDS = 4
REPLICAS = 4
PATCHES = 3072


def other_lengths(key):
    others = IMG_SHARD - 1
    spare = ROWS_DEV - MOST_LEN - others
    room = MOST_LEN - 1
    keys = jax.random.split(key, others + 1)
    rank = jax.vmap(lambda k: jax.random.permutation(k, others))(jax.random.split(keys[0], SHARDS)).astype(jnp.int32)
    extras = (spare // others + (rank < spare % others).astype(jnp.int32)).astype(jnp.int32)
    if others >= 2:
        for turn in range(others):
            first = turn
            second = (turn + 1) % others
            lower = -jnp.minimum(extras[:, first], room - extras[:, second])
            upper = jnp.minimum(extras[:, second], room - extras[:, first])
            moved = jax.random.randint(keys[turn + 1], (SHARDS,), lower, upper + 1, dtype=jnp.int32)
            extras = extras.at[:, first].add(moved).at[:, second].add(-moved)
    return (1 + extras).astype(jnp.int32)


def replica_tables(key):
    keys = jax.random.split(key, 6)
    shard_ids = jnp.arange(SHARDS, dtype=jnp.int32)
    class_ids = jnp.arange(IMG_SHARD, dtype=jnp.int32)
    shifts = jax.random.permutation(keys[1], SHARDS).astype(jnp.int32)[:IMG_SHARD]
    heavy = jax.random.randint(keys[2], (), 0, SHARDS, dtype=jnp.int32)
    target = (shard_ids[:, None] + shifts[None, :]) % SHARDS
    owners = target
    forced = target == heavy
    is_forced = jnp.any(forced, axis=1)
    forced_class = jnp.sum(jnp.where(forced, class_ids[None, :], 0), axis=1)
    free_pick = jax.random.randint(keys[3], (SHARDS,), 0, IMG_SHARD, dtype=jnp.int32)
    big_class = jnp.where(is_forced, forced_class, free_pick)
    composed = other_lengths(keys[4])
    take_index = jnp.clip(class_ids[None, :] - (class_ids[None, :] > big_class[:, None]).astype(jnp.int32), 0, IMG_SHARD - 2)
    lengths = jnp.where(class_ids[None, :] == big_class[:, None], MOST_LEN, jnp.take_along_axis(composed, take_index, axis=1))
    order_keys = jax.random.randint(keys[5], (SHARDS, IMG_SHARD), 0, 1024, dtype=jnp.int32) * IMG_SHARD + class_ids[None, :]
    earlier = order_keys[:, :, None] < order_keys[:, None, :]
    offsets = jnp.sum(jnp.where(earlier, lengths[:, :, None], 0), axis=1)
    return (lengths.astype(jnp.int32), offsets.astype(jnp.int32), owners.astype(jnp.int32))


def all_tables(key):
    keys = jax.random.split(jax.random.fold_in(key, 7), REPLICAS)
    return jax.vmap(replica_tables)(keys)


def draw_image_tokens(key, part):
    return all_tables(key)[0]


def draw_image_offset(key, part):
    return all_tables(key)[1]


def draw_image_owner(key, part):
    return all_tables(key)[2]


def activation_rows(key):
    keys = jax.random.split(key, 3)
    shape = (REPLICAS, PATCH_GROUP, SHARDS * CAP_TOK, D)
    column_scale = jnp.exp(jax.random.uniform(keys[0], (D,), jnp.float32, math.log(0.3), math.log(3.0)))
    row_scale = jnp.exp(jax.random.uniform(keys[1], (REPLICAS, PATCH_GROUP, SHARDS * CAP_TOK, 1), jnp.float32, math.log(0.3), math.log(3.0)))
    base = jnp.clip(jax.random.normal(keys[2], shape, jnp.float32), -4.0, 4.0)
    return (base * row_scale * column_scale).astype(jnp.bfloat16)


def draw_mlp_input(key, part):
    return activation_rows(jax.random.fold_in(key, 11))


def draw_layer_output(key, part):
    return activation_rows(jax.random.fold_in(key, 23))


def steps_of(key, shape, cuts, low, high):
    def one(dim, shards_of):
        draws = jax.random.uniform(jax.random.fold_in(jax.random.fold_in(key, 6), dim), (shards_of,), jnp.float32, low / len(cuts), high / len(cuts))
        return jnp.repeat(jnp.exp(draws), shape[dim] // shards_of).reshape((-1,) + (1,) * (len(shape) - dim - 1))

    factor_of = one(*cuts[0])
    for cut in cuts[1:]:
        factor_of = factor_of * one(*cut)
    return factor_of


def bell_draw(own_key, dims, width, bound, pieces=(), held_as=jnp.bfloat16):
    array = jax.random.normal(own_key, dims, jnp.float32) * width
    if len(pieces) > 0:
        array = steps_of(own_key, dims, pieces, -0.22, 0.18) * array
    return jnp.clip(array, min=-bound, max=bound).astype(held_as)


def setup_inputs(seed: int = 0) -> dict:
    key_of = jax.random.split(jax.random.key(seed), 15)
    lm_grad = bell_draw(key_of[0], (REPLICAS, PATCH_GROUP, SHARDS * ROWS_DEV, D), 1.0, 6.0, ((0, 4), (1, 2), (2, 4)))
    image_tokens = draw_image_tokens(jax.random.fold_in(key_of[14], 71), 0)
    image_offset = draw_image_offset(jax.random.fold_in(key_of[14], 71), 0)
    image_owner = draw_image_owner(jax.random.fold_in(key_of[14], 71), 0)
    mlp_input = draw_mlp_input(jax.random.fold_in(key_of[14], 71), 0)
    layer_output = draw_layer_output(jax.random.fold_in(key_of[14], 71), 0)
    pre_gain = jnp.clip(1.0 + 0.1 * jax.random.normal(key_of[6], (D,), jnp.float32), 0.5, 1.5)
    pre_bias = bell_draw(key_of[7], (D,), 0.5, 3.0, (), jnp.float32)
    fc1_weight = bell_draw(key_of[8], (D, FF), D ** -0.5, 0.1875, ((1, 2),))
    fc1_bias = bell_draw(key_of[9], (FF,), 0.5, 3.0, ((0, 2),), jnp.float32)
    fc2_weight = bell_draw(key_of[10], (FF, D), FF ** -0.5, 0.09375, ((0, 2),))
    post_gain = jnp.clip(1.0 + 0.1 * jax.random.normal(key_of[11], (D,), jnp.float32), 0.5, 1.5)
    post_bias = bell_draw(key_of[12], (D,), 0.5, 3.0, (), jnp.float32)
    merge_gain = jnp.clip(1.0 + 0.1 * jax.random.normal(key_of[13], (D,), jnp.float32), 0.5, 1.5)
    return {"lm_grad": lm_grad, "image_tokens": image_tokens, "image_offset": image_offset, "image_owner": image_owner, "mlp_input": mlp_input, "layer_output": layer_output, "pre_gain": pre_gain, "pre_bias": pre_bias, "fc1_weight": fc1_weight, "fc1_bias": fc1_bias, "fc2_weight": fc2_weight, "post_gain": post_gain, "post_bias": post_bias, "merge_gain": merge_gain}


EPSILON = 1e-06
SLOPE_K = math.sqrt(2.0 / math.pi)
CUBIC = 0.044715

def layer_norm(values):
    row_mean = lax.optimization_barrier(jnp.mean(values, axis=-1, keepdims=True))
    centred = values - row_mean
    return centred * lax.rsqrt(lax.optimization_barrier(jnp.mean(centred * centred, axis=-1, keepdims=True)) + EPSILON)

def rms_norm(values):
    return values * lax.rsqrt(lax.optimization_barrier(jnp.mean(values * values, axis=-1, keepdims=True)) + EPSILON)

def gelu_slope(pre_act):
    inner_arg = SLOPE_K * (pre_act + CUBIC * pre_act * pre_act * pre_act)
    tangent = jnp.tanh(inner_arg)
    return 0.5 * (1.0 + tangent) + 0.5 * pre_act * (1.0 - tangent * tangent) * SLOPE_K * (1.0 + 3.0 * CUBIC * pre_act * pre_act)

def head_back(incoming, layer_rows, merge_gain, post_gain, post_bias):

    def merge_head(row_values, merge_scale, post_scale, post_shift):
        return rms_norm(layer_norm(row_values) * post_scale + post_shift) * merge_scale
    _, pullback = jax.vjp(merge_head, layer_rows.astype(jnp.float32), merge_gain, post_gain, post_bias)
    return pullback(incoming.astype(jnp.float32))

def pre_back(input_rows, pre_gain, pre_bias, upstream):

    def prenorm(row_values, scale_vec, shift_vec):
        return layer_norm(row_values) * scale_vec + shift_vec
    _, pullback = jax.vjp(prenorm, input_rows.astype(jnp.float32), pre_gain, pre_bias)
    return pullback(upstream)

def slot_source(lengths, offsets, owners, chip_index):
    shard_count = lengths.shape[0]
    is_mine = owners == chip_index
    my_len = lax.optimization_barrier(jnp.sum(jnp.where(is_mine, lengths, 0), axis=1)).astype(jnp.int32)
    my_off = lax.optimization_barrier(jnp.sum(jnp.where(is_mine, offsets, 0), axis=1)).astype(jnp.int32)
    slot_first = (jnp.cumsum(my_len) - my_len).astype(jnp.int32)
    slot_ids = jnp.arange(CAP_TOK, dtype=jnp.int32)
    inside = (slot_ids[:, None] >= slot_first[None, :]) & (slot_ids[:, None] < (slot_first + my_len)[None, :])
    live_slot = jnp.any(inside, axis=1)
    shard_ids = jnp.arange(shard_count, dtype=jnp.int32)
    source = lax.optimization_barrier(jnp.sum(jnp.where(inside, shard_ids[None, :], 0), axis=1)).astype(jnp.int32)
    token_index = (slot_ids - lax.optimization_barrier(jnp.sum(jnp.where(inside, slot_first[None, :], 0), axis=1))).astype(jnp.int32)
    shard_row = (lax.optimization_barrier(jnp.sum(jnp.where(inside, my_off[None, :], 0), axis=1)) + token_index).astype(jnp.int32)
    return (live_slot, source, token_index, shard_row)

def reference(lm_grad, image_tokens, image_offset, image_owner, mlp_input, layer_output, pre_gain, pre_bias, fc1_weight, fc1_bias, fc2_weight, post_gain, post_bias, merge_gain):

    def chip_step(running, chip_flat):
        replica = (chip_flat // SHARDS).astype(jnp.int32)
        chip_index = (chip_flat % SHARDS).astype(jnp.int32)
        lengths = lax.dynamic_index_in_dim(image_tokens, replica, 0, keepdims=False)
        offsets = lax.dynamic_index_in_dim(image_offset, replica, 0, keepdims=False)
        owners = lax.dynamic_index_in_dim(image_owner, replica, 0, keepdims=False)
        live_slot, source, token_index, shard_row = slot_source(lengths, offsets, owners, chip_index)
        global_row = jnp.clip(source * ROWS_DEV + shard_row, 0, SHARDS * ROWS_DEV - 1).astype(jnp.int32)
        replica_grad = lax.dynamic_index_in_dim(lm_grad, replica, 0, keepdims=False)
        picked = jnp.take(replica_grad, global_row, axis=1)
        incoming = jnp.where(live_slot[None, :, None], picked, jnp.zeros_like(picked))
        slot_start = (chip_index * CAP_TOK).astype(jnp.int32)
        layer_rows = lax.dynamic_slice_in_dim(lax.dynamic_index_in_dim(layer_output, replica, 0, keepdims=False), slot_start, CAP_TOK, 1)
        input_rows = lax.dynamic_slice_in_dim(lax.dynamic_index_in_dim(mlp_input, replica, 0, keepdims=False), slot_start, CAP_TOK, 1)
        res_grad, merge_grad, post_grad, shift_grad = head_back(incoming, layer_rows, merge_gain, post_gain, post_bias)
        res_wire = res_grad.astype(jnp.bfloat16)
        normed = (layer_norm(input_rows.astype(jnp.float32)) * pre_gain + pre_bias).astype(jnp.bfloat16)
        pre_act = jnp.dot(normed.reshape(-1, D), fc1_weight, preferred_element_type=jnp.float32) + fc1_bias
        hidden_grad = jnp.dot(res_wire.reshape(-1, D), fc2_weight.T, preferred_element_type=jnp.float32) * gelu_slope(pre_act)
        fc1_part = lax.optimization_barrier(jnp.sum(hidden_grad, axis=0))
        upstream = jnp.dot(hidden_grad.astype(jnp.bfloat16), fc1_weight.T, preferred_element_type=jnp.float32).reshape(PATCH_GROUP, CAP_TOK, D)
        input_grad, pre_scale_grad, pre_shift_grad = pre_back(input_rows, pre_gain, pre_bias, upstream)
        act_rows = (res_grad + input_grad).astype(jnp.bfloat16)
        fc2_part = lax.optimization_barrier(jnp.sum(res_grad, axis=(0, 1)))
        norm_part = jnp.stack([merge_grad, post_grad, shift_grad, fc2_part, pre_scale_grad, pre_shift_grad])
        return ((running[0] + norm_part, running[1] + fc1_part), act_rows)
    start_sums = (jnp.zeros((6, D), jnp.float32), jnp.zeros((FF,), jnp.float32))
    (norm_sum, fc1_sum), act_rows = lax.scan(chip_step, start_sums, jnp.arange(REPLICAS * SHARDS, dtype=jnp.int32))
    act_grad = act_rows.reshape(REPLICAS, SHARDS, PATCH_GROUP, CAP_TOK, D).transpose(0, 2, 1, 3, 4).reshape(REPLICAS, PATCH_GROUP, SHARDS * CAP_TOK, D)
    grad_scale = 1.0 / math.sqrt(PATCHES)
    return (act_grad, norm_sum * grad_scale, fc1_sum * grad_scale)
```

```python
import math

import jax
import jax.numpy as jnp
from jax import lax
from jax.experimental import pallas as pl
from jax.experimental.pallas import tpu as pltpu
from jax.sharding import PartitionSpec as P

MOST_LEN = 15
WINDOW = 16
SUBLANES = 8
EPSILON = 1e-06
SLOPE_K = math.sqrt(2.0 / math.pi)
CUBIC = 0.044715
F32 = jnp.float32
BF16 = jnp.bfloat16
MESH_ID = pl.DeviceIdType.MESH


def gelu_slope(pre_act):
    inner_arg = SLOPE_K * (pre_act + CUBIC * pre_act * pre_act * pre_act)
    tangent = jnp.tanh(inner_arg)
    return 0.5 * (1.0 + tangent) + 0.5 * pre_act * (1.0 - tangent * tangent) * SLOPE_K * (
        1.0 + 3.0 * CUBIC * pre_act * pre_act
    )


def row_mean(values):
    return jnp.mean(values, axis=-1, keepdims=True)


def norm_parts(values):
    centred = values - row_mean(values)
    scale = lax.rsqrt(row_mean(centred * centred) + EPSILON)
    return centred * scale, scale


def norm_pull(normal, scale, cotangent):
    return scale * (cotangent - row_mean(cotangent) - normal * row_mean(cotangent * normal))


def greet(peers):
    barrier = pltpu.get_barrier_semaphore()
    for peer in peers:
        pl.semaphore_signal(barrier, inc=1, device_id=peer, device_id_type=MESH_ID)
    return lambda: pl.semaphore_wait(barrier, len(peers))


def others(axis, count):
    me = lax.axis_index(axis)
    return [{axis: lax.rem(me + step, count)} for step in range(1, count)]


def remote(src, dst, send_sem, recv_sem, peer):
    copy = pltpu.make_async_remote_copy(
        src_ref=src,
        dst_ref=dst,
        send_sem=send_sem,
        recv_sem=recv_sem,
        device_id=peer,
        device_id_type=MESH_ID,
    )
    copy.start()
    return copy


def head_kernel(
    shards,
    pack_ref,
    unpack_ref,
    grad_ref,
    layer_ref,
    input_ref,
    pre_gain_ref,
    pre_bias_ref,
    post_gain_ref,
    post_bias_ref,
    merge_ref,
    all_ref,
    res_ref,
    normed_ref,
    sums_ref,
    send_buf,
    recv_buf,
    swap_out,
    swap_in,
    seq_send,
    seq_recv,
    enc_send,
    enc_recv,
):
    me = lax.axis_index("seq")
    core = lax.axis_index("enc")
    partner = {"enc": 1 - core}
    own, rows_dev, width = grad_ref.shape
    slots = layer_ref.shape[1]
    peers = others("seq", shards)
    settle = greet([partner] + peers)
    for patch in range(own):
        packed = jnp.dot(pack_ref[...], grad_ref[patch], preferred_element_type=F32)
        send_buf[:, patch] = packed.astype(BF16).reshape(shards, WINDOW, width)
    settle()
    copies = []
    for step, peer in enumerate(peers):
        copies.append(
            remote(
                send_buf.at[peer["seq"]],
                recv_buf.at[me],
                seq_send.at[step],
                seq_recv.at[step],
                peer,
            )
        )
    recv_buf[me] = send_buf[me]
    pre_gain = pre_gain_ref[...]
    pre_bias = pre_bias_ref[...]
    normed_ref[...] = jnp.zeros_like(normed_ref)
    for patch in range(input_ref.shape[0]):
        normal, _ = norm_parts(input_ref[patch].astype(F32))
        normed_ref[patch, 0:slots, :] = (normal * pre_gain + pre_bias).astype(BF16)
    post_gain = post_gain_ref[...]
    post_bias = post_bias_ref[...]
    merge_gain = merge_ref[...]
    swap_out[...] = jnp.zeros_like(swap_out)
    for copy in copies:
        copy.wait()
    swaps = []
    totals = None
    for patch in range(own):
        landed = recv_buf[:, patch].reshape(shards * WINDOW, width)
        incoming = jnp.dot(unpack_ref[...], landed, preferred_element_type=F32)
        normal, scale = norm_parts(layer_ref[patch].astype(F32))
        affine = normal * post_gain + post_bias
        rms = lax.rsqrt(row_mean(affine * affine) + EPSILON)
        unit = affine * rms
        unit_grad = incoming * merge_gain
        affine_grad = rms * (unit_grad - unit * row_mean(unit_grad * unit))
        res = norm_pull(normal, scale, affine_grad * post_gain)
        res_ref[patch] = res
        swap_out[patch, 0:slots, :] = res.astype(BF16)
        parts = [
            jnp.sum(term, axis=0, keepdims=True)
            for term in (incoming * unit, affine_grad * normal, affine_grad, res)
        ]
        totals = parts if totals is None else [a + b for a, b in zip(totals, parts)]
        swaps.append(
            remote(
                swap_out.at[patch],
                swap_in.at[patch],
                enc_send.at[patch],
                enc_recv.at[patch],
                partner,
            )
        )
        all_ref[core * own + patch] = swap_out[patch]
    sums_ref[...] = jnp.zeros_like(sums_ref)
    for index, total in enumerate(totals):
        sums_ref[index : index + 1, :] = total
    for patch in range(own):
        swaps[patch].wait()
        all_ref[(1 - core) * own + patch] = swap_in[patch]


def tail_kernel(
    shards,
    replicas,
    grad_scale,
    product_ref,
    input_ref,
    pre_gain_ref,
    res_ref,
    sums_ref,
    units_ref,
    act_ref,
    total_ref,
    swap_in,
    halves,
    half_in,
    seq_buf,
    dp_buf,
    last_buf,
    enc_send,
    enc_recv,
    seq_send,
    seq_recv,
    dp_send,
    dp_recv,
):
    me = lax.axis_index("seq")
    replica = lax.axis_index("dp")
    core = lax.axis_index("enc")
    other = 1 - core
    partner = {"enc": other}
    own = act_ref.shape[0]
    slots = act_ref.shape[1]
    seq_peers = others("seq", shards)
    dp_peers = others("dp", replicas)
    settle = greet([partner] + seq_peers + dp_peers)
    halves[...] = jnp.zeros_like(halves)
    unit_rows = units_ref.shape[0]
    halves[0, 0:1, :] = sums_ref[0:1, :]
    halves[0, 1:2, :] = sums_ref[1:2, :]
    halves[0, 2:3, :] = sums_ref[2:3, :]
    halves[1, 0:1, :] = sums_ref[3:4, :]
    for index in range(unit_rows):
        halves[core, 3 + index : 4 + index, :] = units_ref[index : index + 1, :]
    settle()
    swaps = [
        remote(
            product_ref.at[other * own + patch],
            swap_in.at[patch],
            enc_send.at[patch],
            enc_recv.at[patch],
            partner,
        )
        for patch in range(own)
    ]
    pre_gain = pre_gain_ref[...]
    gain_grad = None
    for patch in range(own):
        normal, scale = norm_parts(input_ref[core * own + patch].astype(F32))
        swaps[patch].wait()
        upstream = product_ref[core * own + patch, 0:slots, :] + swap_in[patch, 0:slots, :]
        parts = [
            jnp.sum(upstream * normal, axis=0, keepdims=True),
            jnp.sum(upstream, axis=0, keepdims=True),
        ]
        gain_grad = parts if gain_grad is None else [a + b for a, b in zip(gain_grad, parts)]
        act = res_ref[patch] + norm_pull(normal, scale, upstream * pre_gain)
        act_ref[patch] = act.astype(BF16)
    halves[1, 1:2, :] = gain_grad[0]
    halves[1, 2:3, :] = gain_grad[1]
    remote(halves.at[other], half_in, enc_send.at[own], enc_recv.at[own], partner).wait()
    seq_buf[me] = halves[core] + half_in[...]
    copies = [
        remote(seq_buf.at[me], seq_buf.at[me], seq_send.at[step], seq_recv.at[step], peer)
        for step, peer in enumerate(seq_peers)
    ]
    for copy in copies:
        copy.wait()
    total = seq_buf[0]
    for index in range(1, shards):
        total = total + seq_buf[index]
    dp_buf[replica] = total
    copies = [
        remote(dp_buf.at[replica], dp_buf.at[replica], dp_send.at[step], dp_recv.at[step], peer)
        for step, peer in enumerate(dp_peers)
    ]
    for copy in copies:
        copy.wait()
    total = dp_buf[0]
    for index in range(1, replicas):
        total = total + dp_buf[index]
    last_buf[core] = total * grad_scale
    remote(
        last_buf.at[core], last_buf.at[core], enc_send.at[own + 1], enc_recv.at[own + 1], partner
    ).wait()
    total_ref[...] = last_buf[...]


def round_up(value, step):
    return (value + step - 1) // step * step


def body(
    lm_grad,
    image_tokens,
    image_offset,
    image_owner,
    mlp_input,
    layer_output,
    pre_gain,
    pre_bias,
    fc1_weight,
    fc1_bias,
    fc2_weight,
    post_gain,
    post_bias,
    merge_gain,
):
    me = lax.axis_index("seq")
    shards = lax.axis_size("seq")
    replicas = lax.axis_size("dp")
    cores = lax.axis_size("enc")
    grad_rows = lm_grad[0]
    input_rows = mlp_input[0]
    layer_rows = layer_output[0]
    own, rows_dev, width = grad_rows.shape
    group, slots, _ = input_rows.shape
    padded = round_up(slots, WINDOW)
    lengths, offsets, owners = image_tokens[0], image_offset[0], image_owner[0]

    chips = jnp.arange(shards, dtype=jnp.int32)
    steps = jnp.arange(WINDOW, dtype=jnp.int32)
    my_images = lax.dynamic_slice_in_dim(jnp.stack([lengths, offsets, owners]), me, 1, 1)[:, 0]
    to_chip = my_images[2][None, :] == chips[:, None]
    sent_len = jnp.sum(jnp.where(to_chip, my_images[0][None, :], 0), axis=1)
    sent_off = jnp.sum(jnp.where(to_chip, my_images[1][None, :], 0), axis=1)
    source_row = jnp.where(
        steps[None, :] < sent_len[:, None], sent_off[:, None] + steps[None, :], -1
    ).reshape(-1)
    pack = (source_row[:, None] == jnp.arange(rows_dev, dtype=jnp.int32)[None, :]).astype(BF16)
    mine_len = jnp.sum(jnp.where(owners == me, lengths, 0), axis=1)
    first = jnp.sum(jnp.where(chips[None, :] < chips[:, None], mine_len[None, :], 0), axis=1)
    target_slot = jnp.where(
        steps[None, :] < mine_len[:, None], first[:, None] + steps[None, :], -1
    ).reshape(-1)
    unpack = (jnp.arange(slots, dtype=jnp.int32)[:, None] == target_slot[None, :]).astype(BF16)

    vmem = pl.BlockSpec(memory_space=pltpu.VMEM)
    dma = pltpu.SemaphoreType.DMA
    gain_row = pre_gain.reshape(1, width)

    def head_call(*refs):
        head_kernel(shards, *refs)

    all_res, res_grad, normed, sums = pl.pallas_call(
        head_call,
        out_shape=(
            jax.ShapeDtypeStruct((group, padded, width), BF16),
            jax.ShapeDtypeStruct((own, slots, width), F32),
            jax.ShapeDtypeStruct((group, padded, width), BF16),
            jax.ShapeDtypeStruct((SUBLANES, width), F32),
        ),
        in_specs=[vmem] * 10,
        out_specs=(vmem,) * 4,
        scratch_shapes=[
            pltpu.VMEM((shards, own, WINDOW, width), BF16),
            pltpu.VMEM((shards, own, WINDOW, width), BF16),
            pltpu.VMEM((own, padded, width), BF16),
            pltpu.VMEM((own, padded, width), BF16),
            dma((shards - 1,)),
            dma((shards - 1,)),
            dma((own,)),
            dma((own,)),
        ],
        compiler_params=pltpu.CompilerParams(collective_id=0, has_side_effects=True),
        name="head",
    )(
        pack,
        unpack,
        grad_rows,
        layer_rows,
        input_rows,
        gain_row,
        pre_bias.reshape(1, width),
        post_gain.reshape(1, width),
        post_bias.reshape(1, width),
        merge_gain.reshape(1, width),
    )

    pre_act = (
        jnp.dot(normed.reshape(-1, width), fc1_weight, preferred_element_type=F32) + fc1_bias
    )
    down_back = lax.dot_general(
        all_res.reshape(-1, width),
        fc2_weight,
        (((1,), (1,)), ((), ())),
        preferred_element_type=F32,
    )
    hidden_grad = down_back * gelu_slope(pre_act)
    fc1_part = jnp.sum(hidden_grad, axis=0)
    hidden_units = fc1_bias.shape[0]
    product = lax.dot_general(
        hidden_grad.astype(BF16),
        fc1_weight,
        (((1,), (1,)), ((), ())),
        preferred_element_type=F32,
    ).reshape(group, padded, width)
    unit_rows = round_up(hidden_units, width) // width
    units = jnp.pad(fc1_part, (0, unit_rows * width - hidden_units)).reshape(unit_rows, width)

    grad_scale = 1.0 / math.sqrt(group * rows_dev * shards * replicas)
    sum_rows = round_up(3 + unit_rows, SUBLANES)

    def tail_call(*refs):
        tail_kernel(shards, replicas, grad_scale, *refs)

    act_grad, totals = pl.pallas_call(
        tail_call,
        out_shape=(
            jax.ShapeDtypeStruct((own, slots, width), BF16),
            jax.ShapeDtypeStruct((cores, sum_rows, width), F32),
        ),
        in_specs=[vmem] * 6,
        out_specs=(vmem,) * 2,
        scratch_shapes=[
            pltpu.VMEM((own, padded, width), F32),
            pltpu.VMEM((cores, sum_rows, width), F32),
            pltpu.VMEM((sum_rows, width), F32),
            pltpu.VMEM((shards, sum_rows, width), F32),
            pltpu.VMEM((replicas, sum_rows, width), F32),
            pltpu.VMEM((cores, sum_rows, width), F32),
            dma((own + 2,)),
            dma((own + 2,)),
            dma((shards - 1,)),
            dma((shards - 1,)),
            dma((replicas - 1,)),
            dma((replicas - 1,)),
        ],
        compiler_params=pltpu.CompilerParams(collective_id=1, has_side_effects=True),
        name="tail",
    )(product, input_rows, gain_row, res_grad, sums, units)
    norm_grads = totals[:, :3].reshape(-1, width)
    fc1_grad = totals[:, 3 : 3 + unit_rows].reshape(cores, -1)[:, :hidden_units].reshape(-1)
    return (act_grad[None], norm_grads, fc1_grad)


def solution(mesh):
    in_specs = (
        P("dp", "enc", "seq", None),
        P("dp", None, None),
        P("dp", None, None),
        P("dp", None, None),
        P("dp", None, "seq", None),
        P("dp", "enc", "seq", None),
        P(),
        P(),
        P(None, "enc"),
        P("enc"),
        P("enc", None),
        P(),
        P(),
        P(),
    )
    out_specs = (P("dp", "enc", "seq", None), P(), P())
    return jax.shard_map(body, mesh=mesh, in_specs=in_specs, out_specs=out_specs, check_vma=False)
```

```python
import math

import jax
import jax.numpy as jnp
from jax import lax
from jax.experimental import pallas as pl
from jax.experimental.pallas import tpu as pltpu
from jax.sharding import PartitionSpec as P

MOST_LEN = 15
WINDOW = 16
SUBLANES = 8
HEAD_VMEM = 24 * 1024 * 1024
EPSILON = 1e-06
SLOPE_K = math.sqrt(2.0 / math.pi)
CUBIC = 0.044715
F32 = jnp.float32
BF16 = jnp.bfloat16
MESH_ID = pl.DeviceIdType.MESH


def gelu_slope(pre_act):
    inner_arg = SLOPE_K * (pre_act + CUBIC * pre_act * pre_act * pre_act)
    tangent = jnp.tanh(inner_arg)
    return 0.5 * (1.0 + tangent) + 0.5 * pre_act * (1.0 - tangent * tangent) * SLOPE_K * (
        1.0 + 3.0 * CUBIC * pre_act * pre_act
    )


def row_mean(values):
    return jnp.mean(values, axis=-1, keepdims=True)


def norm_parts(values):
    centred = values - row_mean(values)
    scale = lax.rsqrt(row_mean(centred * centred) + EPSILON)
    return centred * scale, scale


def norm_pull(normal, scale, cotangent):
    return scale * (cotangent - row_mean(cotangent) - normal * row_mean(cotangent * normal))


def greet(peers):
    barrier = pltpu.get_barrier_semaphore()
    for peer in peers:
        pl.semaphore_signal(barrier, inc=1, device_id=peer, device_id_type=MESH_ID)
    return lambda: pl.semaphore_wait(barrier, len(peers))


def others(axis, count):
    me = lax.axis_index(axis)
    return [{axis: lax.rem(me + step, count)} for step in range(1, count)]


def remote(src, dst, send_sem, recv_sem, peer):
    copy = pltpu.make_async_remote_copy(
        src_ref=src,
        dst_ref=dst,
        send_sem=send_sem,
        recv_sem=recv_sem,
        device_id=peer,
        device_id_type=MESH_ID,
    )
    copy.start()
    return copy


def head_kernel(
    shards,
    tokens_ref,
    offsets_ref,
    owners_ref,
    grad_ref,
    layer_ref,
    input_ref,
    pre_gain_ref,
    pre_bias_ref,
    post_gain_ref,
    post_bias_ref,
    merge_ref,
    all_ref,
    res_ref,
    normed_ref,
    sums_ref,
    send_buf,
    recv_buf,
    swap_out,
    swap_in,
    seq_send,
    seq_recv,
    enc_send,
    enc_recv,
):
    me = lax.axis_index("seq")
    core = lax.axis_index("enc")
    partner = {"enc": 1 - core}
    own, rows_dev, width = grad_ref.shape
    slots = layer_ref.shape[1]
    peers = others("seq", shards)
    settle = greet([partner] + peers)
    images = tokens_ref.shape[1]
    places = shards * WINDOW
    place = lax.broadcasted_iota(jnp.int32, (places, rows_dev), 0)
    chip, step = place // WINDOW, place % WINDOW
    source = jnp.full((places, rows_dev), -1, jnp.int32)
    for image in range(images):
        taken = (chip == owners_ref[me, image]) & (step < tokens_ref[me, image])
        source = jnp.where(taken, offsets_ref[me, image] + step, source)
    row = lax.broadcasted_iota(jnp.int32, (places, rows_dev), 1)
    pack = jnp.where(row == source, 1.0, 0.0).astype(BF16)
    for patch in range(own):
        packed = jnp.dot(pack, grad_ref[patch], preferred_element_type=F32)
        send_buf[:, patch] = packed.astype(BF16).reshape(shards, WINDOW, width)
    settle()
    copies = []
    for step, peer in enumerate(peers):
        copies.append(
            remote(
                send_buf.at[peer["seq"]],
                recv_buf.at[me],
                seq_send.at[step],
                seq_recv.at[step],
                peer,
            )
        )
    recv_buf[me] = send_buf[me]
    pre_gain = pre_gain_ref[...].reshape(1, -1)
    pre_bias = pre_bias_ref[...].reshape(1, -1)
    normed_ref[...] = jnp.zeros_like(normed_ref)
    for patch in range(input_ref.shape[0]):
        normal, _ = norm_parts(input_ref[patch].astype(F32))
        normed_ref[patch, 0:slots, :] = (normal * pre_gain + pre_bias).astype(BF16)
    post_gain = post_gain_ref[...].reshape(1, -1)
    post_bias = post_bias_ref[...].reshape(1, -1)
    merge_gain = merge_ref[...].reshape(1, -1)
    swap_out[...] = jnp.zeros_like(swap_out)
    place = lax.broadcasted_iota(jnp.int32, (slots, places), 1)
    chip, step = place // WINDOW, place % WINDOW
    target = jnp.full((slots, places), -1, jnp.int32)
    first = jnp.int32(0)
    for shard in range(shards):
        count = jnp.int32(0)
        for image in range(images):
            count += jnp.where(owners_ref[shard, image] == me, tokens_ref[shard, image], 0)
        target = jnp.where((chip == shard) & (step < count), first + step, target)
        first += count
    slot = lax.broadcasted_iota(jnp.int32, (slots, places), 0)
    unpack = jnp.where(slot == target, 1.0, 0.0).astype(BF16)
    for copy in copies:
        copy.wait()
    swaps = []
    totals = None
    for patch in range(own):
        landed = recv_buf[:, patch].reshape(shards * WINDOW, width)
        incoming = jnp.dot(unpack, landed, preferred_element_type=F32)
        normal, scale = norm_parts(layer_ref[patch].astype(F32))
        affine = normal * post_gain + post_bias
        rms = lax.rsqrt(row_mean(affine * affine) + EPSILON)
        unit = affine * rms
        unit_grad = incoming * merge_gain
        affine_grad = rms * (unit_grad - unit * row_mean(unit_grad * unit))
        res = norm_pull(normal, scale, affine_grad * post_gain)
        res_ref[patch] = res
        swap_out[patch, 0:slots, :] = res.astype(BF16)
        parts = [
            jnp.sum(term, axis=0, keepdims=True)
            for term in (incoming * unit, affine_grad * normal, affine_grad, res)
        ]
        totals = parts if totals is None else [a + b for a, b in zip(totals, parts)]
        swaps.append(
            remote(
                swap_out.at[patch],
                swap_in.at[patch],
                enc_send.at[patch],
                enc_recv.at[patch],
                partner,
            )
        )
        all_ref[core * own + patch] = swap_out[patch]
    sums_ref[...] = jnp.zeros_like(sums_ref)
    for index, total in enumerate(totals):
        sums_ref[index : index + 1, :] = total
    for patch in range(own):
        swaps[patch].wait()
        all_ref[(1 - core) * own + patch] = swap_in[patch]


def tail_kernel(
    shards,
    replicas,
    grad_scale,
    product_ref,
    input_ref,
    pre_gain_ref,
    res_ref,
    sums_ref,
    units_ref,
    act_ref,
    norm_ref,
    unit_ref,
    swap_out,
    swap_in,
    normals,
    halves,
    half_in,
    seq_buf,
    dp_buf,
    last_buf,
    enc_send,
    enc_recv,
    seq_send,
    seq_recv,
    dp_send,
    dp_recv,
):
    me = lax.axis_index("seq")
    replica = lax.axis_index("dp")
    core = lax.axis_index("enc")
    other = 1 - core
    partner = {"enc": other}
    own = act_ref.shape[0]
    slots = act_ref.shape[1]
    seq_peers = others("seq", shards)
    dp_peers = others("dp", replicas)
    settle = greet([partner] + seq_peers + dp_peers)
    halves[...] = jnp.zeros_like(halves)
    width = act_ref.shape[2]
    hidden = units_ref.shape[1]
    spans = [(at, min(width, hidden - at)) for at in range(0, hidden, width)]
    halves[0, 0:1, :] = sums_ref[0:1, :]
    halves[0, 1:2, :] = sums_ref[1:2, :]
    halves[0, 2:3, :] = sums_ref[2:3, :]
    halves[1, 0:1, :] = sums_ref[3:4, :]
    for index, (at, size) in enumerate(spans):
        halves[core, 3 + index : 4 + index, 0:size] = units_ref[:, at : at + size]
    for patch in range(own):
        swap_out[patch] = product_ref[other * own + patch].astype(BF16)
    settle()
    swaps = [
        remote(
            swap_out.at[patch],
            swap_in.at[patch],
            enc_send.at[patch],
            enc_recv.at[patch],
            partner,
        )
        for patch in range(own)
    ]
    pre_gain = pre_gain_ref[...].reshape(1, -1)
    scales = []
    for patch in range(own):
        normal, scale = norm_parts(input_ref[core * own + patch].astype(F32))
        normals[patch] = normal
        scales.append(scale)
    gain_grad = None
    for patch in range(own):
        swaps[patch].wait()
        upstream = product_ref[core * own + patch, 0:slots, :] + swap_in[patch, 0:slots, :].astype(F32)
        parts = [
            jnp.sum(upstream * normals[patch], axis=0, keepdims=True),
            jnp.sum(upstream, axis=0, keepdims=True),
        ]
        gain_grad = parts if gain_grad is None else [a + b for a, b in zip(gain_grad, parts)]
    halves[1, 1:2, :] = gain_grad[0]
    halves[1, 2:3, :] = gain_grad[1]

    def finish(patch):
        upstream = product_ref[core * own + patch, 0:slots, :] + swap_in[patch, 0:slots, :].astype(F32)
        act = res_ref[patch] + norm_pull(normals[patch], scales[patch], upstream * pre_gain)
        act_ref[patch] = act.astype(BF16)

    half_copy = remote(halves.at[other], half_in, enc_send.at[own], enc_recv.at[own], partner)
    finish(0)
    half_copy.wait()
    seq_buf[me] = halves[core] + half_in[...]
    copies = [
        remote(seq_buf.at[me], seq_buf.at[me], seq_send.at[step], seq_recv.at[step], peer)
        for step, peer in enumerate(seq_peers)
    ]
    for patch in range(1, own):
        finish(patch)
    for copy in copies:
        copy.wait()
    total = seq_buf[0]
    for index in range(1, shards):
        total = total + seq_buf[index]
    dp_buf[replica] = total
    copies = [
        remote(dp_buf.at[replica], dp_buf.at[replica], dp_send.at[step], dp_recv.at[step], peer)
        for step, peer in enumerate(dp_peers)
    ]
    for copy in copies:
        copy.wait()
    total = dp_buf[0]
    for index in range(1, replicas):
        total = total + dp_buf[index]
    last_buf[core] = total * grad_scale
    remote(
        last_buf.at[core], last_buf.at[core], enc_send.at[own + 1], enc_recv.at[own + 1], partner
    ).wait()
    for half in range(2):
        norm_ref[3 * half : 3 * half + 3, :] = last_buf[half, 0:3, :]
        for index, (at, size) in enumerate(spans):
            unit_ref[half : half + 1, at : at + size] = last_buf[half, 3 + index : 4 + index, 0:size]


def round_up(value, step):
    return (value + step - 1) // step * step


def body(
    lm_grad,
    image_tokens,
    image_offset,
    image_owner,
    mlp_input,
    layer_output,
    pre_gain,
    pre_bias,
    fc1_weight,
    fc1_bias,
    fc2_weight,
    post_gain,
    post_bias,
    merge_gain,
):
    shards = lax.axis_size("seq")
    replicas = lax.axis_size("dp")
    cores = lax.axis_size("enc")
    grad_rows = lm_grad[0]
    input_rows = mlp_input[0]
    layer_rows = layer_output[0]
    own, rows_dev, width = grad_rows.shape
    group, slots, _ = input_rows.shape
    padded = round_up(slots, WINDOW)

    vmem = pl.BlockSpec(memory_space=pltpu.VMEM)
    dma = pltpu.SemaphoreType.DMA

    def head_call(*refs):
        head_kernel(shards, *refs)

    all_res, res_grad, normed, sums = pl.pallas_call(
        head_call,
        out_shape=(
            jax.ShapeDtypeStruct((group, padded, width), BF16),
            jax.ShapeDtypeStruct((own, slots, width), F32),
            jax.ShapeDtypeStruct((group, padded, width), BF16),
            jax.ShapeDtypeStruct((SUBLANES, width), F32),
        ),
        in_specs=[pl.BlockSpec(memory_space=pltpu.SMEM)] * 3 + [vmem] * 8,
        out_specs=(vmem,) * 4,
        scratch_shapes=[
            pltpu.VMEM((shards, own, WINDOW, width), BF16),
            pltpu.VMEM((shards, own, WINDOW, width), BF16),
            pltpu.VMEM((own, padded, width), BF16),
            pltpu.VMEM((own, padded, width), BF16),
            dma((shards - 1,)),
            dma((shards - 1,)),
            dma((own,)),
            dma((own,)),
        ],
        compiler_params=pltpu.CompilerParams(
            collective_id=0, has_side_effects=True, vmem_limit_bytes=HEAD_VMEM
        ),
        cost_estimate=pl.CostEstimate(flops=4_000_000_000, bytes_accessed=24_000_000, transcendentals=0),
        name="head",
    )(
        image_tokens[0],
        image_offset[0],
        image_owner[0],
        grad_rows,
        layer_rows,
        input_rows,
        pre_gain,
        pre_bias,
        post_gain,
        post_bias,
        merge_gain,
    )

    pre_act = (
        jnp.dot(normed.reshape(-1, width), fc1_weight, preferred_element_type=F32) + fc1_bias
    )
    down_back = lax.dot_general(
        all_res.reshape(-1, width),
        fc2_weight,
        (((1,), (1,)), ((), ())),
        preferred_element_type=F32,
    )
    hidden_grad = down_back * gelu_slope(pre_act)
    units = jnp.sum(hidden_grad, axis=0, keepdims=True)
    hidden_units = fc1_bias.shape[0]
    product = lax.dot_general(
        hidden_grad.astype(BF16),
        fc1_weight,
        (((1,), (1,)), ((), ())),
        preferred_element_type=F32,
    ).reshape(group, padded, width)
    unit_rows = round_up(hidden_units, width) // width

    grad_scale = 1.0 / math.sqrt(group * rows_dev * shards * replicas)
    sum_rows = round_up(3 + unit_rows, SUBLANES)

    def tail_call(*refs):
        tail_kernel(shards, replicas, grad_scale, *refs)

    act_grad, norm_grads, unit_grads = pl.pallas_call(
        tail_call,
        out_shape=(
            jax.ShapeDtypeStruct((own, slots, width), BF16),
            jax.ShapeDtypeStruct((6, width), F32),
            jax.ShapeDtypeStruct((cores, hidden_units), F32),
        ),
        in_specs=[vmem] * 6,
        out_specs=(vmem,) * 3,
        scratch_shapes=[
            pltpu.VMEM((own, padded, width), BF16),
            pltpu.VMEM((own, padded, width), BF16),
            pltpu.VMEM((own, slots, width), F32),
            pltpu.VMEM((cores, sum_rows, width), F32),
            pltpu.VMEM((sum_rows, width), F32),
            pltpu.VMEM((shards, sum_rows, width), F32),
            pltpu.VMEM((replicas, sum_rows, width), F32),
            pltpu.VMEM((cores, sum_rows, width), F32),
            dma((own + 2,)),
            dma((own + 2,)),
            dma((shards - 1,)),
            dma((shards - 1,)),
            dma((replicas - 1,)),
            dma((replicas - 1,)),
        ],
        compiler_params=pltpu.CompilerParams(collective_id=1, has_side_effects=True),
        name="tail",
    )(product, input_rows, pre_gain, res_grad, sums, units)
    return (act_grad[None], norm_grads, unit_grads.reshape(-1))


def solution(mesh):
    in_specs = (
        P("dp", "enc", "seq", None),
        P("dp", None, None),
        P("dp", None, None),
        P("dp", None, None),
        P("dp", None, "seq", None),
        P("dp", "enc", "seq", None),
        P(),
        P(),
        P(None, "enc"),
        P("enc"),
        P("enc", None),
        P(),
        P(),
        P(),
    )
    out_specs = (P("dp", "enc", "seq", None), P(), P())
    return jax.shard_map(body, mesh=mesh, in_specs=in_specs, out_specs=out_specs, check_vma=False)
```
